512 devices in a mesh: row: 32 (over x_lo, y, core), col: 16 (over z, x_hi).
Axes of the slice: x: 4 (x_hi: 2, x_lo: 2; x = x_hi * 2 + x_lo), y: 8, z: 8, core: 2. Of those that a mesh axis runs over, the one named last changes fastest.
Arguments:
- support: bfloat16 [131072, 4096], P(('row', 'col')), may hold values from -6 to 6
- targets: bfloat16 [1024, 4096], P('col'), may hold values from -6 to 6
- panels: float32 [2, 128, 131072], P(None, None, ('row', 'col')), may hold values from -0.21875 to 0.21875
- diag_inverses: float32 [2, 128, 128], replicated, may hold values from -1 to 1.5, as said below
Outputs:
- solved: float32 [1024, 131072], P('col', 'row')
The draws below stay inside these ranges and needn't reach their ends.
Inputs may be any that keep to these rules, and one draw needn't show every extreme that they name: Each diag_inverses[k] is lower triangular.
All inputs are finite; a program needn't handle non-finite values.
Results may differ from the reference program's by a relative error of at most 0.0003.
Values may be sent and summed in bfloat16 or wider, within the bound.
A program may use at most 64 MiB of HBM per device.

```python
import math
import jax
import jax.numpy as jnp
from jax import lax

FEAT = 4096
PANEL = 128
ROWS_DEV = 256
SUPPORT = 131072
TARGETS = 1024
N_ROW = 32
N_COL = 16


def feature_draw(key, count):
    values = jax.random.truncated_normal(key, -6.0, 6.0, (count, FEAT), jnp.float32)
    return values.astype(jnp.bfloat16)


def draw_support(key, part):
    return feature_draw(jax.random.fold_in(key, 3), SUPPORT)


def draw_targets(key, part):
    return feature_draw(jax.random.fold_in(key, 7), TARGETS)


def draw_diag_inverses(key, part):
    first_key, second_key = jax.random.split(jax.random.fold_in(key, 11))
    lower = jnp.tril(jnp.ones((PANEL, PANEL), jnp.float32), -1)
    identity = jnp.eye(PANEL, dtype=jnp.float32)
    spread = 0.5 * jax.random.truncated_normal(first_key, -4.0, 4.0, (2, PANEL, PANEL), jnp.float32)
    diagonal = jax.random.uniform(second_key, (2, PANEL, PANEL), jnp.float32, 0.6, 1.4)
    return lower * spread * (1.0 / math.sqrt(PANEL)) + identity * diagonal


def block_scale(stream_key, dims, cuts, smallest, largest):
    loudness, own = 1.0, jax.random.fold_in(stream_key, 6)
    for position, blocks in cuts:
        steps = jnp.exp(jax.random.uniform(jax.random.fold_in(own, position), (blocks,), jnp.float32, smallest / len(cuts), largest / len(cuts)))
        loudness = loudness * jnp.repeat(steps, dims[position] // blocks).reshape([-1 if axis == position else 1 for axis in range(len(dims))])
    return loudness


def noise(rng, dims, deviation, bound, shards=(), kind=jnp.bfloat16):
    level = block_scale(rng, dims, shards, -0.22, 0.18) if shards else 1.0
    array = jax.random.normal(rng, dims, jnp.float32) * deviation * level
    return jnp.minimum(jnp.maximum(array, -bound), bound).astype(kind)


def setup_inputs(seed: int = 0) -> dict:
    splits = jax.random.split(jax.random.key(seed), 5)
    support = draw_support(jax.random.fold_in(splits[4], 71), 0)
    targets = draw_targets(jax.random.fold_in(splits[4], 71), 0)
    panels = noise(splits[2], (2, PANEL, SUPPORT), (6 * PANEL) ** -0.5, 0.21875, ((2, 512),), jnp.float32)
    diag_inverses = draw_diag_inverses(jax.random.fold_in(splits[4], 71), 0)
    return {"support": support, "targets": targets, "panels": panels, "diag_inverses": diag_inverses}


def reference(support, targets, panels, diag_inverses):
    feature_width = support.shape[1]
    kernel_scale = 0.5 / math.sqrt(feature_width)
    grid_span = ROWS_DEV * N_COL
    pivot_width = diag_inverses.shape[1]

    def form_block(support_rows):
        products = jnp.dot(targets, support_rows.T, preferred_element_type=jnp.float32)
        return jnp.exp(kernel_scale * products)
    blocks = support.reshape(N_ROW, grid_span, feature_width)
    kernel = lax.map(form_block, blocks)
    kernel = jnp.transpose(kernel, (1, 0, 2)).reshape(targets.shape[0], support.shape[0])
    for panel_num in range(2):
        lower = panel_num * grid_span
        kept_heads = [kernel[:, earlier * grid_span:earlier * grid_span + pivot_width] for earlier in range(panel_num)]
        pivot_cols = kernel[:, lower:lower + pivot_width]
        solved_head = jnp.dot(pivot_cols, diag_inverses[panel_num].T, precision=lax.Precision.HIGHEST, preferred_element_type=jnp.float32)
        kernel = kernel - jnp.dot(solved_head, panels[panel_num], precision=lax.Precision.HIGHEST, preferred_element_type=jnp.float32)
        kernel = kernel.at[:, lower:lower + pivot_width].set(solved_head)
        for earlier in range(panel_num):
            kernel = kernel.at[:, earlier * grid_span:earlier * grid_span + pivot_width].set(kept_heads[earlier])
    return kernel
```

```python
import math

import jax
import jax.numpy as jnp
from jax import lax
from jax.experimental import pallas as pl
from jax.experimental.pallas import tpu as pltpu
from jax.sharding import PartitionSpec as P

MESH = pl.DeviceIdType.MESH
NZ, NY, NX = 8, 8, 4
BAND = 16
HIGH = lax.Precision.HIGHEST


def dot_t(a, b, precision=None):
    return lax.dot_general(
        a, b, (((1,), (1,)), ((), ())), precision=precision, preferred_element_type=jnp.float32
    )


def body(
    scale, sup, tgt, pan, inv, out,
    full, piv, cross_pan, kern, sol,
    full_recv, z_send, cross_send, part_send, sib_send,
    piv_own, piv_z, piv_x, piv_b, root_send, y_send, pz_send, px_send, pb_send,
    pan_own, pan_z, pan_b, rootp_send, yp_send, pzp_send, pbp_send,
    out_recv, out_send,
):
    row = lax.axis_index("row")
    col = lax.axis_index("col")
    core = row % 2
    y = (row // 2) % NY
    x_lo = row // (2 * NY)
    z = col // 2
    x_hi = col % 2
    x = x_hi * 2 + x_lo
    quarter = sup.shape[1] // NX

    def dev(xx, yy, zz, kk):
        return ((xx % 2) * (2 * NY) + yy * 2 + kk, zz * 2 + xx // 2)

    sibling = dev(x, y, z, 1 - core)
    crossing = dev(NX - 1 - x, y, z, core)
    partner = dev(x_hi * 2 + 1 - x_lo, y, z, core)

    def copy(src, dst, send, recv, to):
        return pltpu.make_async_remote_copy(
            src_ref=src, dst_ref=dst, send_sem=send, recv_sem=recv, device_id=to, device_id_type=MESH
        )

    barrier = pltpu.get_barrier_semaphore()

    def greet_plane(i, carry):
        other = (z * NX + x + i) % (NZ * NX)
        pl.semaphore_signal(
            barrier, inc=1, device_id=dev(other % NX, y, other // NX, core), device_id_type=MESH
        )
        return carry

    def greet_line(i, carry):
        pl.semaphore_signal(
            barrier, inc=1, device_id=dev(x, (y + i) % NY, z, core), device_id_type=MESH
        )
        return carry

    lax.fori_loop(1, NZ * NX, greet_plane, 0)
    lax.fori_loop(1, NY, greet_line, 0)
    pl.semaphore_signal(barrier, inc=1, device_id=sibling, device_id_type=MESH)
    pl.semaphore_wait(barrier, NZ * NX - 1 + NY - 1 + 1)

    def band(ref, index):
        return ref.at[pl.ds(pl.multiple_of(index * BAND, BAND), BAND), :]

    def piece(zz, xh, kk, q):
        return (((zz + 2 * NZ) % NZ) * 2 + xh) * 4 + kk * 2 + q

    def held(p):
        return band(full, p)

    def arrived(p):
        copy(held(p), held(p), sib_send.at[p], full_recv.at[p], sibling).wait_recv()

    def share(p):
        copy(held(p), held(p), sib_send.at[p], full_recv.at[p], sibling).start()

    def ahead(t, p, src):
        return copy(src, held(p), z_send.at[0, t], full_recv.at[p], dev(x, y, (z + 1) % NZ, core))

    def behind(t, p, src):
        return copy(src, held(p), z_send.at[1, t], full_recv.at[p], dev(x, y, (z + NZ - 1) % NZ, core))

    def over(t, p, src):
        return copy(src, held(p), cross_send.at[t], full_recv.at[p], crossing)

    def hand(t, p):
        return copy(held(p), held(p), part_send.at[t], full_recv.at[p], partner)

    is_root = (x == 0) & (y == 0) & (z == 0)

    def piv_block(kk, xx, zz):
        return piv.at[kk, xx, pl.ds(pl.multiple_of(zz * BAND, BAND), BAND), :]

    def pan_block(kk, zz):
        return cross_pan.at[kk, pl.ds(pl.multiple_of(zz * BAND, BAND), BAND), :]

    def sup_block(xx, zz):
        return sup.at[
            pl.ds(pl.multiple_of(zz * BAND, BAND), BAND),
            pl.ds(pl.multiple_of(xx * quarter, quarter), quarter),
        ]

    def pan_src(zz):
        return pan.at[0, pl.ds(pl.multiple_of(zz * BAND, BAND), BAND), pl.ds(0, pan.shape[1])]

    def root_copies(i):
        xx, zz = i % NX, i // NX
        to = dev(xx, y, zz, core)
        return (
            copy(sup_block(xx, zz), piv_block(core, xx, zz), root_send.at[i], piv_own, to),
            copy(pan_src(zz), pan_block(core, zz), rootp_send.at[i], pan_own, to),
        )

    def y_copies(i):
        to = dev(x, (y + i) % NY, z, core)
        return (
            copy(piv_block(core, x, z), piv_block(core, x, z), y_send.at[i], piv_own, to),
            copy(pan_block(core, z), pan_block(core, z), yp_send.at[i], pan_own, to),
        )

    def z_copies(i):
        to = dev(x, y, (z + i) % NZ, core)
        return (
            copy(piv_block(core, x, z), piv_block(core, x, z), pz_send.at[i], piv_z.at[z], to),
            copy(pan_block(core, z), pan_block(core, z), pzp_send.at[i], pan_z.at[z], to),
        )

    def x_copy(i):
        xx = (x + i) % NX
        return copy(piv.at[core, x], piv.at[core, x], px_send.at[i], piv_x.at[x], dev(xx, y, z, core))

    def b_copy(xx):
        return copy(piv.at[core, xx], piv.at[core, xx], pb_send.at[xx], piv_b.at[xx], sibling)

    def bp_copy():
        return copy(cross_pan.at[core], cross_pan.at[core], pbp_send, pan_b, sibling)

    def each(first, last, make, act):
        def step(i, carry):
            made = make(i)
            for one in made if isinstance(made, tuple) else (made,):
                act(one)
            return carry

        lax.fori_loop(first, last, step, 0)

    @pl.when(is_root)
    def _():
        each(1, NZ * NX, root_copies, lambda c: c.start())
        pltpu.make_async_copy(sup_block(0, 0), piv_block(core, 0, 0), piv_own).start()
        pltpu.make_async_copy(pan_src(0), pan_block(core, 0), pan_own).start()

    ahead(0, piece(z, x_hi, core, 0), band(tgt, core * 2)).start()
    behind(0, piece(z, x_hi, core, 1), band(tgt, core * 2 + 1)).start()
    over(0, piece(z, x_hi, core, x_lo), band(tgt, core * 2 + x_lo)).start()
    mine = tgt.shape[0]
    full[pl.ds(pl.multiple_of(col * mine, mine), mine), :] = tgt[...]
    side = 2 * x_lo - 1

    def come_over(t):
        return piece(z - side * t, 1 - x_hi, core, 1 - x_lo)

    def come_by(t):
        return piece(z + side * t, 1 - x_hi, core, x_lo)

    def take_over(t):
        p = come_over(t)
        arrived(p)
        hand(t, p).start()
        share(p)

    def take_by(t):
        p = come_by(t)
        arrived(p)
        share(p)

    def ring(t, carry):
        p0 = piece(z - t, x_hi, core, 0)
        p1 = piece(z + t, x_hi, core, 1)
        arrived(p0)

        @pl.when(t < NZ - 1)
        def _():
            ahead(t, p0, held(p0)).start()

        arrived(p1)

        @pl.when(t < NZ - 1)
        def _():
            behind(t, p1, held(p1)).start()

        pc = piece(z + side * t, x_hi, core, x_lo)
        over(t, pc, held(pc)).start()
        share(p0)
        share(p1)
        take_over(t - 1)

        @pl.when(t >= 2)
        def _():
            take_by(t - 2)

        return carry

    lax.fori_loop(1, 4, ring, 0)

    own_piv = copy(piv_block(core, x, z), piv_block(core, x, z), y_send.at[0], piv_own, sibling)
    own_pan = copy(pan_block(core, z), pan_block(core, z), yp_send.at[0], pan_own, sibling)

    @pl.when(y == 0)
    def _():
        own_piv.wait_recv()
        own_pan.wait_recv()
        each(1, NY, y_copies, lambda c: c.start())

    lax.fori_loop(4, 6, ring, 0)

    @pl.when(y > 0)
    def _():
        own_piv.wait_recv()
        own_pan.wait_recv()

    each(1, NZ, z_copies, lambda c: c.start())
    lax.fori_loop(6, NZ, ring, 0)
    take_over(NZ - 1)
    take_by(NZ - 2)
    take_by(NZ - 1)

    def from_z(i):
        zz = (z + i) % NZ
        return (
            copy(piv_block(core, x, zz), piv_block(core, x, zz), pz_send.at[i], piv_z.at[zz], sibling),
            copy(pan_block(core, zz), pan_block(core, zz), pzp_send.at[i], pan_z.at[zz], sibling),
        )

    each(1, NZ, from_z, lambda c: c.wait_recv())
    each(1, NX, x_copy, lambda c: c.start())
    b_copy(x).start()
    bp_copy().start()

    def sibling_target(i, carry):
        s = (col + i) % (2 * NZ)
        arrived(s * 4 + (1 - core) * 2)
        arrived(s * 4 + (1 - core) * 2 + 1)
        return carry

    lax.fori_loop(1, 2 * NZ, sibling_target, 0)

    chunk = 256
    chunks = full.shape[0] // chunk

    def rows_of(i):
        return pl.ds(pl.multiple_of(i * chunk, chunk), chunk)

    def strip(i, carry):
        kern[rows_of(i), :] = jnp.exp(scale * dot_t(full[rows_of(i), :], sup[...]))
        return carry

    lax.fori_loop(0, chunks, strip, 0)

    def from_x(i):
        xx = (x + i) % NX
        copy(piv.at[core, xx], piv.at[core, xx], px_send.at[i], piv_x.at[xx], sibling).wait_recv()
        return b_copy(xx)

    each(1, NX, from_x, lambda c: c.start())

    def from_b(xx):
        return copy(piv.at[1 - core, xx], piv.at[1 - core, xx], pb_send.at[xx], piv_b.at[xx], sibling)

    each(0, NX, from_b, lambda c: c.wait_recv())
    copy(cross_pan.at[1 - core], cross_pan.at[1 - core], pbp_send, pan_b, sibling).wait_recv()

    width = inv.shape[1]
    span = sup.shape[0]
    here = pl.ds(pl.multiple_of(col * span, span), span)

    def out_copy(c):
        return copy(
            sol.at[pl.ds(pl.multiple_of(c * mine, mine), mine), :],
            out.at[:, here], out_send.at[c], out_recv.at[col], (row, c),
        )

    def solve(i, carry):
        number = (z // 2 + 2 + i) % chunks
        these = rows_of(number)

        def pivot_kernel(kk):
            total = jnp.zeros((chunk, width), jnp.float32)
            for xx in range(NX):
                total += dot_t(full[these, xx * quarter : (xx + 1) * quarter], piv[kk, xx])
            return jnp.exp(scale * total)

        first = dot_t(pivot_kernel(0), inv[0], HIGH)
        left = pivot_kernel(1) - jnp.dot(
            first, cross_pan[1], precision=HIGH, preferred_element_type=jnp.float32
        )
        second = dot_t(left, inv[1], HIGH)
        done = (
            kern[these, :]
            - jnp.dot(first, pan[0], precision=HIGH, preferred_element_type=jnp.float32)
            - jnp.dot(second, pan[1], precision=HIGH, preferred_element_type=jnp.float32)
        )
        head = jnp.where(
            (row == 0) & (col == 0), first,
            jnp.where((row == 1) & (col == 0), second, done[:, :width]),
        )
        sol[these, :width] = head
        sol[these, width:] = done[:, width:]
        for j in range(chunk // mine):
            c = number * (chunk // mine) + j

            @pl.when(c != col)
            def _():
                out_copy(c).start()

            @pl.when(c == col)
            def _():
                pltpu.make_async_copy(
                    sol.at[pl.ds(pl.multiple_of(c * mine, mine), mine), :],
                    out.at[:, here], out_recv.at[col],
                ).start()

        return carry

    lax.fori_loop(0, chunks, solve, 0)

    def end_ring(t, carry):
        ahead(t, 0, held(0)).wait_send()
        behind(t, 0, held(0)).wait_send()
        return carry

    lax.fori_loop(0, NZ - 1, end_ring, 0)

    def end_x(t, carry):
        over(t, 0, held(0)).wait_send()
        hand(t, 0).wait_send()
        return carry

    lax.fori_loop(0, NZ, end_x, 0)

    def end_share(i, carry):
        s = (col + i) % (2 * NZ)
        for q in range(2):
            p = s * 4 + core * 2 + q
            copy(held(p), held(p), sib_send.at[p], full_recv.at[p], sibling).wait_send()
        return carry

    lax.fori_loop(1, 2 * NZ, end_share, 0)

    @pl.when(is_root)
    def _():
        each(1, NZ * NX, root_copies, lambda c: c.wait_send())

    @pl.when(y == 0)
    def _():
        each(1, NY, y_copies, lambda c: c.wait_send())

    each(1, NZ, z_copies, lambda c: c.wait_send())
    each(1, NX, x_copy, lambda c: c.wait_send())
    each(0, NX, b_copy, lambda c: c.wait_send())
    bp_copy().wait_send()

    def end_out(i, carry):
        c = (col + i) % (2 * NZ)
        out_copy(c).wait_send()
        copy(
            sol.at[pl.ds(0, mine), :],
            out.at[:, pl.ds(pl.multiple_of(c * span, span), span)],
            out_send.at[c], out_recv.at[c], (row, c),
        ).wait_recv()
        return carry

    lax.fori_loop(1, 2 * NZ, end_out, 0)
    pltpu.make_async_copy(
        sol.at[pl.ds(pl.multiple_of(col * mine, mine), mine), :], out.at[:, here], out_recv.at[col]
    ).wait()


def shards(support, targets, panels, diag_inverses):
    span, feat = support.shape
    mine = targets.shape[0]
    width = diag_inverses.shape[1]
    n_col = 2 * NZ
    scale = 0.5 / math.sqrt(feat)
    dma = pltpu.SemaphoreType.DMA

    def kernel(*refs):
        body(scale, *refs)

    return pl.pallas_call(
        kernel,
        out_shape=jax.ShapeDtypeStruct((mine, span * n_col), jnp.float32),
        in_specs=[pl.BlockSpec(memory_space=pltpu.VMEM)] * 4,
        out_specs=pl.BlockSpec(memory_space=pl.ANY),
        scratch_shapes=[
            pltpu.VMEM((mine * n_col, feat), jnp.bfloat16),
            pltpu.VMEM((2, NX, width, feat // NX), jnp.bfloat16),
            pltpu.VMEM((2, width, width), jnp.float32),
            pltpu.VMEM((mine * n_col, span), jnp.float32),
            pltpu.VMEM((mine * n_col, span), jnp.float32),
            dma((4 * n_col,)), dma((2, NZ)), dma((NZ,)), dma((NZ,)), dma((4 * n_col,)),
            dma, dma((NZ,)), dma((NX,)), dma((NX,)),
            dma((NZ * NX,)), dma((NY,)), dma((NZ,)), dma((NX,)), dma((NX,)),
            dma, dma((NZ,)), dma, dma((NZ * NX,)), dma((NY,)), dma((NZ,)), dma,
            dma((n_col,)), dma((n_col,)),
        ],
        compiler_params=pltpu.CompilerParams(
            collective_id=0, has_side_effects=True, vmem_limit_bytes=48 * 1024 * 1024
        ),
    )(support, targets, panels, diag_inverses)


def solution(mesh):
    in_specs = (P(("row", "col"), None), P("col", None), P(None, None, ("row", "col")), P())
    out_specs = P("col", "row")
    return jax.shard_map(shards, mesh=mesh, in_specs=in_specs, out_specs=out_specs, check_vma=False)
```

```python
import functools
import math

import jax
import jax.numpy as jnp
from jax import lax
from jax.experimental import pallas as pl
from jax.experimental.pallas import tpu as pltpu
from jax.sharding import PartitionSpec as P

MESH = pl.DeviceIdType.MESH
NZ, NY, NX = 8, 8, 4
BAND = 16
STEP_ROWS = 256
BEGIN_AT, FIRST_AT, OTHER_AT, LINE_AT, LINE_STEPS = 6, 8, 9, 12, (14, 16, 100, 101)
HIGH = lax.Precision.HIGHEST


def dot_t(a, b, precision=None):
    return lax.dot_general(
        a, b, (((1,), (1,)), ((), ())), precision=precision, preferred_element_type=jnp.float32
    )


def body(
    scale, sup_hbm, tgt, pan_hbm, inv_hbm, out,
    sup, pan, inv, full, piv, cross_pan, kern, sol,
    load, full_recv, z_send, cross_send, part_send, sib_send,
    landed, stage_recv, line_send, linep_send,
    piv_own, piv_z, piv_y, piv_b, root_send, px_send, pz_send, py_send, pb_send,
    pan_own, pan_z, pan_b, rootp_send, pxp_send, pzp_send, pbp_send,
    out_recv, out_send,
):
    row = lax.axis_index("row")
    col = lax.axis_index("col")
    core = row % 2
    y = (row // 2) % NY
    x_lo = row // (2 * NY)
    z = col // 2
    x_hi = col % 2
    x = x_hi * 2 + x_lo
    part = sup.shape[1] // NY
    half = sup.shape[1] // 2
    width = inv.shape[1]

    def dev(xx, yy, zz, kk):
        return ((xx % 2) * (2 * NY) + yy * 2 + kk, zz * 2 + xx // 2)

    sibling = dev(x, y, z, 1 - core)
    crossing = dev(NX - 1 - x, y, z, core)
    partner = dev(x_hi * 2 + 1 - x_lo, y, z, core)

    def copy(src, dst, send, recv, to):
        return pltpu.make_async_remote_copy(
            src_ref=src, dst_ref=dst, send_sem=send, recv_sem=recv, device_id=to, device_id_type=MESH
        )

    mine = tgt.shape[0]
    loads = [
        pltpu.make_async_copy(sup_hbm, sup, load.at[0]),
        pltpu.make_async_copy(pan_hbm, pan, load.at[1]),
        pltpu.make_async_copy(inv_hbm, inv, load.at[2]),
        pltpu.make_async_copy(tgt, full.at[pl.ds(pl.multiple_of(col * mine, mine), mine), :], load.at[3]),
    ]
    for one in loads:
        one.start()

    def first_x(zz):
        return (zz % 2) * (zz % NX)

    is_root = (x == 0) & (y == 0) & (z == 0)
    is_first = x == first_x(z)

    barrier = pltpu.get_barrier_semaphore()

    def greet_plane(i, carry):
        other = (z * NX + x + i) % (NZ * NX)
        pl.semaphore_signal(
            barrier, inc=1, device_id=dev(other % NX, y, other // NX, core), device_id_type=MESH
        )
        return carry

    def greet_line(i, carry):
        pl.semaphore_signal(
            barrier, inc=1, device_id=dev(x, (y + i) % NY, z, core), device_id_type=MESH
        )
        return carry

    lax.fori_loop(1, NZ * NX, greet_plane, 0)
    lax.fori_loop(1, NY, greet_line, 0)
    pl.semaphore_signal(barrier, inc=1, device_id=sibling, device_id_type=MESH)

    pl.semaphore_wait(barrier, NZ * NX - 1 + NY - 1 + 1)

    def band(ref, index, c):
        return ref.at[pl.ds(pl.multiple_of(index * BAND, BAND), BAND), pl.ds(pl.multiple_of(c * half, half), half)]

    def piece(zz, xh, kk, q):
        return (((zz + 2 * NZ) % NZ) * 2 + xh) * 4 + kk * 2 + q

    def held(p, c):
        return band(full, p, c)

    def sib(p, c):
        return copy(held(p, c), held(p, c), sib_send.at[p, c], full_recv.at[p, c], sibling)

    def arrived(p, c):
        sib(p, c).wait_recv()

    def share(p, c):
        sib(p, c).start()

    def ahead(t, p, c, src):
        return copy(src, held(p, c), z_send.at[0, t, c], full_recv.at[p, c], dev(x, y, (z + 1) % NZ, core))

    def behind(t, p, c, src):
        return copy(src, held(p, c), z_send.at[1, t, c], full_recv.at[p, c], dev(x, y, (z + NZ - 1) % NZ, core))

    def over(t, p, c, src):
        return copy(src, held(p, c), cross_send.at[t, c], full_recv.at[p, c], crossing)

    def hand(t, p, c):
        return copy(held(p, c), held(p, c), part_send.at[t, c], full_recv.at[p, c], partner)

    def piv_block(kk, yy, zz):
        return piv.at[yy, pl.ds(pl.multiple_of(kk * width + zz * BAND, BAND), BAND), :]

    def pan_block(kk, zz):
        return cross_pan.at[kk, pl.ds(pl.multiple_of(zz * BAND, BAND), BAND), :]

    def sup_band(zz):
        return sup_hbm.at[pl.ds(pl.multiple_of(zz * BAND, BAND), BAND), :]

    def staged(yy):
        return landed.at[:, pl.ds(pl.multiple_of(yy * part, part), part)]

    def pan_src(zz):
        return pan_hbm.at[0, pl.ds(pl.multiple_of(zz * BAND, BAND), BAND), pl.ds(0, inv.shape[1])]

    def root_copy(zz):
        return copy(sup_band(zz), landed, root_send.at[zz], stage_recv, dev(first_x(zz), 0, zz, core))

    def rootp_copy(zz):
        return copy(pan_src(zz), pan_block(core, zz), rootp_send.at[zz], pan_own, dev(first_x(zz), 0, zz, core))

    def line_copy(i):
        return copy(staged(i), piv_block(core, i, z), line_send.at[i], piv_own, dev(x, i, z, core))

    def linep_copy(i):
        return copy(pan_block(core, z), pan_block(core, z), linep_send.at[i], pan_own, dev(x, i, z, core))

    def x_copy(i):
        to = dev((x + i) % NX, y, z, core)
        return copy(piv_block(core, y, z), piv_block(core, y, z), px_send.at[i], piv_own, to)

    def xp_copy(i):
        to = dev((x + i) % NX, y, z, core)
        return copy(pan_block(core, z), pan_block(core, z), pxp_send.at[i], pan_own, to)

    def z_copy(i):
        to = dev(x, y, (z + i) % NZ, core)
        return copy(piv_block(core, y, z), piv_block(core, y, z), pz_send.at[i], piv_z.at[z], to)

    def zp_copy(i):
        to = dev(x, y, (z + i) % NZ, core)
        return copy(pan_block(core, z), pan_block(core, z), pzp_send.at[i], pan_z.at[z], to)

    hb = width // 2

    def piv_half(kk, yy, c):
        return piv.at[yy, pl.ds(pl.multiple_of(kk * width + c * hb, hb), hb), :]

    def y_copy(way, t, c):
        yy = (y + NY - t) % NY if way == 0 else (y + t) % NY
        to = dev(x, (y + 1) % NY if way == 0 else (y + NY - 1) % NY, z, core)
        return copy(piv_half(core, yy, c), piv_half(core, yy, c), py_send.at[way, t, c], piv_y.at[yy, c], to)

    def b_copy(yy, c):
        return copy(piv_half(core, yy, c), piv_half(core, yy, c), pb_send.at[yy, c], piv_b.at[yy, c], sibling)

    def bp_copy():
        return copy(cross_pan.at[core], cross_pan.at[core], pbp_send, pan_b, sibling)

    def each(first, last, make, act):
        def step(i, carry):
            made = make(i)
            for one in made if isinstance(made, tuple) else (made,):
                act(one)
            return carry

        lax.fori_loop(first, last, step, 0)

    @pl.when(is_root)
    def _():
        each(1, NZ, root_copy, lambda c: c.start())
        pltpu.make_async_copy(sup_band(0), landed, stage_recv).start()
        each(1, NZ, rootp_copy, lambda c: c.start())
        pltpu.make_async_copy(pan_src(0), pan_block(core, 0), pan_own).start()

    for c in range(2):
        ahead(0, piece(z, x_hi, core, 0), c, band(tgt, core * 2, c)).start()
        behind(0, piece(z, x_hi, core, 1), c, band(tgt, core * 2 + 1, c)).start()
        over(0, piece(z, x_hi, core, x_lo), c, band(tgt, core * 2 + x_lo, c)).start()
    side = 2 * x_lo - 1

    def take_over(t, c):
        p = piece(z - side * t, 1 - x_hi, core, 1 - x_lo)
        arrived(p, c)
        hand(t, p, c).start()
        share(p, c)

    def take_by(t, c):
        p = piece(z + side * t, 1 - x_hi, core, x_lo)
        arrived(p, c)
        share(p, c)

    def ring(u, carry):
        t, c = u // 2, u % 2
        p0 = piece(z - t, x_hi, core, 0)
        p1 = piece(z + t, x_hi, core, 1)
        arrived(p0, c)

        @pl.when(t < NZ - 1)
        def _():
            ahead(t, p0, c, held(p0, c)).start()

        arrived(p1, c)

        @pl.when(t < NZ - 1)
        def _():
            behind(t, p1, c, held(p1, c)).start()

        pc = piece(z + side * t, x_hi, core, x_lo)
        over(t, pc, c, held(pc, c)).start()
        share(p0, c)
        share(p1, c)
        take_over(t - 1, c)

        @pl.when(t >= 2)
        def _():
            take_by(t - 2, c)

        return carry

    own_piv = copy(piv_block(core, y, z), piv_block(core, y, z), px_send.at[0], piv_own, sibling)
    own_pan = copy(pan_block(core, z), pan_block(core, z), pxp_send.at[0], pan_own, sibling)

    def stage_begin():
        @pl.when(is_first & (y == 0))
        def _():
            pltpu.make_async_copy(sup_band(0), landed, stage_recv).wait()
            each(1, NY, line_copy, lambda c: c.start())
            pltpu.make_async_copy(staged(0), piv_block(core, 0, z), piv_own).start()
            own_pan.wait_recv()
            each(1, NY, linep_copy, lambda c: c.start())

    def stage_first():
        @pl.when(is_first)
        def _():
            own_piv.wait_recv()
            each(1, NX, x_copy, lambda c: c.start())
            each(1, NZ, z_copy, lambda c: c.start())

    def stage_other():
        @pl.when(x != first_x(z))
        def _():
            own_piv.wait_recv()
            each(1, NZ, z_copy, lambda c: c.start())

    def from_z(i):
        zz = (z + i) % NZ
        return copy(piv_block(core, y, zz), piv_block(core, y, zz), pz_send.at[i], piv_z.at[zz], sibling)

    def fromp_z(i):
        zz = (z + i) % NZ
        return copy(pan_block(core, zz), pan_block(core, zz), pzp_send.at[i], pan_z.at[zz], sibling)

    def stage_line():
        each(1, NZ, from_z, lambda c: c.wait_recv())
        for c in range(2):
            y_copy(0, 0, c).start()
            y_copy(1, 0, c).start()
        for c in range(2):
            b_copy(y, c).start()

        @pl.when(is_first & (y > 0))
        def _():
            own_pan.wait_recv()

        @pl.when(is_first)
        def _():
            each(1, NX, xp_copy, lambda c: c.start())

        @pl.when(x != first_x(z))
        def _():
            own_pan.wait_recv()

        each(1, NZ, zp_copy, lambda c: c.start())

    def y_step(t):
        for c in range(2):
            for way in range(2):
                if t < NY // 2 or c == way:
                    one = y_copy(way, t, c)
                    one.wait_recv()
                    if t < NY // 2 - 1 or (t == NY // 2 - 1 and c == way):
                        one.start()
                    b_copy((y + NY - t) % NY if way == 0 else (y + t) % NY, c).start()

    def ring_end(u):
        t, c = u // 2, u % 2
        take_over(t - 1, c)
        take_by(t - 2, c)

    stages = [(BEGIN_AT, stage_begin), (FIRST_AT, stage_first), (OTHER_AT, stage_other), (LINE_AT, stage_line)]
    stages += [(at, functools.partial(y_step, 1 + n)) for n, at in enumerate(LINE_STEPS)]
    done = 2
    for at, stage in sorted(stages, key=lambda one: one[0]):
        upto = min(at, 2 * NZ)
        if upto > done:
            lax.fori_loop(done, upto, lambda u, carry: ring(u, carry), 0)
            done = upto
        while done < at:
            if done < 2 * NZ + 2:
                ring_end(done)
            done += 1
        if at < 100:
            stage()
    for u in range(done, 2 * NZ + 2):
        ring_end(u)
    for c in range(2):
        take_by(NZ - 1, c)

    def sibling_target(i, carry):
        s = (col + i) % (2 * NZ)
        for q in range(2):
            for c in range(2):
                arrived(s * 4 + (1 - core) * 2 + q, c)
        return carry

    lax.fori_loop(1, 2 * NZ, sibling_target, 0)
    for one in loads:
        one.wait()

    chunk = 256
    chunks = full.shape[0] // chunk

    def rows_of(i):
        return pl.ds(pl.multiple_of(i * chunk, chunk), chunk)

    def strip(i, carry):
        kern[rows_of(i), :] = jnp.exp(scale * dot_t(full[rows_of(i), :], sup[...]))
        return carry

    def from_b(yy, c):
        return copy(piv_half(1 - core, yy, c), piv_half(1 - core, yy, c), pb_send.at[yy, c], piv_b.at[yy, c], sibling)

    for i in range(chunks):
        for n, at in enumerate(LINE_STEPS):
            if at == 100 + i:
                y_step(1 + n)
        strip(i, 0)
    each(1, NZ, fromp_z, lambda c: c.wait_recv())
    bp_copy().start()
    each(0, 2 * NY, lambda i: from_b(i // 2, i % 2), lambda c: c.wait_recv())
    copy(cross_pan.at[1 - core], cross_pan.at[1 - core], pbp_send, pan_b, sibling).wait_recv()

    span = sup.shape[0]
    here = pl.ds(pl.multiple_of(col * span, span), span)

    def out_copy(c):
        return copy(
            sol.at[pl.ds(pl.multiple_of(c * mine, mine), mine), :],
            out.at[:, here], out_send.at[c], out_recv.at[col], (row, c),
        )

    step_rows = STEP_ROWS
    steps = full.shape[0] // step_rows

    def solve(i, carry):
        number = (z * 2 * mine // step_rows + steps // 2 + i) % steps
        these = pl.ds(pl.multiple_of(number * step_rows, step_rows), step_rows)

        total = jnp.zeros((step_rows, 2 * width), jnp.float32)
        for yy in range(NY):
            total += dot_t(full[these, yy * part : (yy + 1) * part], piv[yy])
        pivots = jnp.exp(scale * total)
        first = dot_t(pivots[:, :width], inv[0], HIGH)
        left = pivots[:, width:] - jnp.dot(
            first, cross_pan[1], precision=HIGH, preferred_element_type=jnp.float32
        )
        second = dot_t(left, inv[1], HIGH)
        done = (
            kern[these, :]
            - jnp.dot(
                jnp.concatenate([first, second], axis=1), pan[...].reshape(2 * width, span),
                precision=HIGH, preferred_element_type=jnp.float32,
            )
        )
        head = jnp.where(
            (row == 0) & (col == 0), first,
            jnp.where((row == 1) & (col == 0), second, done[:, :width]),
        )
        sol[these, :width] = head
        sol[these, width:] = done[:, width:]
        for j in range(step_rows // mine):
            c = number * (step_rows // mine) + j

            @pl.when(c != col)
            def _():
                out_copy(c).start()

            @pl.when(c == col)
            def _():
                pltpu.make_async_copy(
                    sol.at[pl.ds(pl.multiple_of(c * mine, mine), mine), :],
                    out.at[:, here], out_recv.at[col],
                ).start()

        return carry

    lax.fori_loop(0, steps, solve, 0)

    def end_ring(u, carry):
        t, c = u // 2, u % 2
        ahead(t, 0, c, held(0, c)).wait_send()
        behind(t, 0, c, held(0, c)).wait_send()
        return carry

    lax.fori_loop(0, 2 * NZ - 2, end_ring, 0)

    def end_x(u, carry):
        t, c = u // 2, u % 2
        over(t, 0, c, held(0, c)).wait_send()
        hand(t, 0, c).wait_send()
        return carry

    lax.fori_loop(0, 2 * NZ, end_x, 0)

    def end_share(i, carry):
        s = (col + i) % (2 * NZ)
        for q in range(2):
            for c in range(2):
                sib(s * 4 + core * 2 + q, c).wait_send()
        return carry

    lax.fori_loop(1, 2 * NZ, end_share, 0)

    @pl.when(is_root)
    def _():
        each(1, NZ, root_copy, lambda c: c.wait_send())
        each(1, NZ, rootp_copy, lambda c: c.wait_send())

    @pl.when(is_first & (y == 0))
    def _():
        each(1, NY, line_copy, lambda c: c.wait_send())
        each(1, NY, linep_copy, lambda c: c.wait_send())

    @pl.when(is_first)
    def _():
        each(1, NX, x_copy, lambda c: c.wait_send())
        each(1, NX, xp_copy, lambda c: c.wait_send())

    each(1, NZ, z_copy, lambda c: c.wait_send())
    each(1, NZ, zp_copy, lambda c: c.wait_send())
    for t in range(NY // 2):
        for c in range(2):
            for way in range(2):
                if t < NY // 2 - 1 or c == way:
                    y_copy(way, t, c).wait_send()
    each(0, 2 * NY, lambda i: b_copy(i // 2, i % 2), lambda c: c.wait_send())
    bp_copy().wait_send()

    def end_out(i, carry):
        c = (col + i) % (2 * NZ)
        out_copy(c).wait_send()
        copy(
            sol.at[pl.ds(0, mine), :],
            out.at[:, pl.ds(pl.multiple_of(c * span, span), span)],
            out_send.at[c], out_recv.at[c], (row, c),
        ).wait_recv()
        return carry

    lax.fori_loop(1, 2 * NZ, end_out, 0)
    pltpu.make_async_copy(
        sol.at[pl.ds(pl.multiple_of(col * mine, mine), mine), :], out.at[:, here], out_recv.at[col]
    ).wait()


def shards(support, targets, panels, diag_inverses):
    span, feat = support.shape
    mine = targets.shape[0]
    width = diag_inverses.shape[1]
    n_col = 2 * NZ
    scale = 0.5 / math.sqrt(feat)
    dma = pltpu.SemaphoreType.DMA

    def kernel(*refs):
        body(scale, *refs)

    return pl.pallas_call(
        kernel,
        out_shape=jax.ShapeDtypeStruct((mine, span * n_col), jnp.float32),
        in_specs=[pl.BlockSpec(memory_space=pltpu.HBM)] * 4,
        out_specs=pl.BlockSpec(memory_space=pltpu.HBM),
        scratch_shapes=[
            pltpu.VMEM(support.shape, support.dtype),
            pltpu.VMEM(panels.shape, panels.dtype),
            pltpu.VMEM(diag_inverses.shape, diag_inverses.dtype),
            pltpu.VMEM((mine * n_col, feat), jnp.bfloat16),
            pltpu.VMEM((NY, 2 * width, feat // NY), jnp.bfloat16),
            pltpu.VMEM((2, width, width), jnp.float32),
            pltpu.VMEM((mine * n_col, span), jnp.float32),
            pltpu.VMEM((mine * n_col, span), jnp.float32),
            dma((4,)), dma((4 * n_col, 2)), dma((2, NZ, 2)), dma((NZ, 2)), dma((NZ, 2)), dma((4 * n_col, 2)),
            pltpu.VMEM((BAND, feat), jnp.bfloat16), dma, dma((NY,)), dma((NY,)),
            dma, dma((NZ,)), dma((NY, 2)), dma((NY, 2)),
            dma((NZ,)), dma((NX,)), dma((NZ,)), dma((2, NY, 2)), dma((NY, 2)),
            dma, dma((NZ,)), dma, dma((NZ,)), dma((NX,)), dma((NZ,)), dma,
            dma((n_col,)), dma((n_col,)),
        ],
        compiler_params=pltpu.CompilerParams(
            collective_id=0, has_side_effects=True, vmem_limit_bytes=67_000_000
        ),
    )(support, targets, panels, diag_inverses)


def solution(mesh):
    in_specs = (P(("row", "col"), None), P("col", None), P(None, None, ("row", "col")), P())
    out_specs = P("col", "row")
    return jax.shard_map(shards, mesh=mesh, in_specs=in_specs, out_specs=out_specs, check_vma=False)
```

```python
import functools
import math

import jax
import jax.numpy as jnp
from jax import lax
from jax.experimental import pallas as pl
from jax.experimental.pallas import tpu as pltpu
from jax.sharding import PartitionSpec as P

MESH = pl.DeviceIdType.MESH
NZ, NY, NX = 8, 8, 4
BAND = 16
STEP_ROWS = 256
BEGIN_AT, FIRST_AT, OTHER_AT, LINE_AT, LINE_STEPS = 6, 8, 9, 12, (14, 16, 100, 101)
HIGH = lax.Precision.HIGHEST


def dot_t(a, b, precision=None):
    return lax.dot_general(
        a, b, (((1,), (1,)), ((), ())), precision=precision, preferred_element_type=jnp.float32
    )


def body(
    scale, sup_hbm, tgt, pan_hbm, inv_hbm, out,
    sup, pan, inv, full, piv, cross_pan, kern, sol,
    load, full_recv, z_send, cross_send, part_send, sib_send,
    landed, stage_recv, line_send, linep_send,
    piv_own, piv_z, piv_y, piv_b, root_send, px_send, pz_send, py_send, pb_send,
    pan_own, pan_z, pan_b, rootp_send, pxp_send, pzp_send, pbp_send,
    out_recv, out_send,
):
    row = lax.axis_index("row")
    col = lax.axis_index("col")
    core = row % 2
    y = (row // 2) % NY
    x_lo = row // (2 * NY)
    z = col // 2
    x_hi = col % 2
    x = x_hi * 2 + x_lo
    part = sup.shape[1] // NY
    half = sup.shape[1] // 2
    width = inv.shape[1]

    def dev(xx, yy, zz, kk):
        return ((xx % 2) * (2 * NY) + yy * 2 + kk, zz * 2 + xx // 2)

    sibling = dev(x, y, z, 1 - core)
    crossing = dev(NX - 1 - x, y, z, core)
    partner = dev(x_hi * 2 + 1 - x_lo, y, z, core)

    def copy(src, dst, send, recv, to):
        return pltpu.make_async_remote_copy(
            src_ref=src, dst_ref=dst, send_sem=send, recv_sem=recv, device_id=to, device_id_type=MESH
        )

    mine = tgt.shape[0]
    loads = [
        pltpu.make_async_copy(sup_hbm, sup, load.at[0]),
        pltpu.make_async_copy(pan_hbm, pan, load.at[1]),
        pltpu.make_async_copy(inv_hbm, inv, load.at[2]),
        pltpu.make_async_copy(tgt, full.at[pl.ds(pl.multiple_of(col * mine, mine), mine), :], load.at[3]),
    ]
    for one in loads:
        one.start()

    def first_x(zz):
        return (zz % 2) * (zz % NX)

    is_root = (x == 0) & (y == 0) & (z == 0)
    is_first = x == first_x(z)

    barrier = pltpu.get_barrier_semaphore()

    def greet_plane(i, carry):
        other = (z * NX + x + i) % (NZ * NX)
        pl.semaphore_signal(
            barrier, inc=1, device_id=dev(other % NX, y, other // NX, core), device_id_type=MESH
        )
        return carry

    def greet_line(i, carry):
        pl.semaphore_signal(
            barrier, inc=1, device_id=dev(x, (y + i) % NY, z, core), device_id_type=MESH
        )
        return carry

    lax.fori_loop(1, NZ * NX, greet_plane, 0)
    lax.fori_loop(1, NY, greet_line, 0)
    pl.semaphore_signal(barrier, inc=1, device_id=sibling, device_id_type=MESH)

    pl.semaphore_wait(barrier, NZ * NX - 1 + NY - 1 + 1)

    def band(ref, index, c):
        return ref.at[pl.ds(pl.multiple_of(index * BAND, BAND), BAND), pl.ds(pl.multiple_of(c * half, half), half)]

    def piece(zz, xh, kk, q):
        return (((zz + 2 * NZ) % NZ) * 2 + xh) * 4 + kk * 2 + q

    def held(p, c):
        return band(full, p, c)

    def sib(p, c):
        return copy(held(p, c), held(p, c), sib_send.at[p, c], full_recv.at[p, c], sibling)

    def arrived(p, c):
        sib(p, c).wait_recv()

    def share(p, c):
        sib(p, c).start()

    def ahead(t, p, c, src):
        return copy(src, held(p, c), z_send.at[0, t, c], full_recv.at[p, c], dev(x, y, (z + 1) % NZ, core))

    def behind(t, p, c, src):
        return copy(src, held(p, c), z_send.at[1, t, c], full_recv.at[p, c], dev(x, y, (z + NZ - 1) % NZ, core))

    def over(t, p, c, src):
        return copy(src, held(p, c), cross_send.at[t, c], full_recv.at[p, c], crossing)

    def hand(t, p, c):
        return copy(held(p, c), held(p, c), part_send.at[t, c], full_recv.at[p, c], partner)

    def piv_block(kk, yy, zz):
        return piv.at[yy, pl.ds(pl.multiple_of(kk * width + zz * BAND, BAND), BAND), :]

    def pan_block(kk, zz):
        return cross_pan.at[kk, pl.ds(pl.multiple_of(zz * BAND, BAND), BAND), :]

    def sup_band(zz):
        return sup_hbm.at[pl.ds(pl.multiple_of(zz * BAND, BAND), BAND), :]

    def staged(yy):
        return landed.at[:, pl.ds(pl.multiple_of(yy * part, part), part)]

    def pan_src(zz):
        return pan_hbm.at[0, pl.ds(pl.multiple_of(zz * BAND, BAND), BAND), pl.ds(0, inv.shape[1])]

    def root_copy(zz):
        return copy(sup_band(zz), landed, root_send.at[zz], stage_recv, dev(first_x(zz), 0, zz, core))

    def rootp_copy(zz):
        return copy(pan_src(zz), pan_block(core, zz), rootp_send.at[zz], pan_own, dev(first_x(zz), 0, zz, core))

    def line_copy(i):
        return copy(staged(i), piv_block(core, i, z), line_send.at[i], piv_own, dev(x, i, z, core))

    def linep_copy(i):
        return copy(pan_block(core, z), pan_block(core, z), linep_send.at[i], pan_own, dev(x, i, z, core))

    def x_copy(i):
        to = dev((x + i) % NX, y, z, core)
        return copy(piv_block(core, y, z), piv_block(core, y, z), px_send.at[i], piv_own, to)

    def xp_copy(i):
        to = dev((x + i) % NX, y, z, core)
        return copy(pan_block(core, z), pan_block(core, z), pxp_send.at[i], pan_own, to)

    def z_copy(i):
        to = dev(x, y, (z + i) % NZ, core)
        return copy(piv_block(core, y, z), piv_block(core, y, z), pz_send.at[i], piv_z.at[z], to)

    def zp_copy(i):
        to = dev(x, y, (z + i) % NZ, core)
        return copy(pan_block(core, z), pan_block(core, z), pzp_send.at[i], pan_z.at[z], to)

    hb = width // 2

    def piv_half(kk, yy, c):
        return piv.at[yy, pl.ds(pl.multiple_of(kk * width + c * hb, hb), hb), :]

    def y_copy(way, t, c):
        yy = (y + NY - t) % NY if way == 0 else (y + t) % NY
        to = dev(x, (y + 1) % NY if way == 0 else (y + NY - 1) % NY, z, core)
        return copy(piv_half(core, yy, c), piv_half(core, yy, c), py_send.at[way, t, c], piv_y.at[yy, c], to)

    def b_copy(yy, c):
        return copy(piv_half(core, yy, c), piv_half(core, yy, c), pb_send.at[yy, c], piv_b.at[yy, c], sibling)

    def bp_copy():
        return copy(cross_pan.at[core], cross_pan.at[core], pbp_send, pan_b, sibling)

    def each(first, last, make, act):
        def step(i, carry):
            made = make(i)
            for one in made if isinstance(made, tuple) else (made,):
                act(one)
            return carry

        lax.fori_loop(first, last, step, 0)

    @pl.when(is_root)
    def _():
        each(1, NZ, root_copy, lambda c: c.start())
        pltpu.make_async_copy(sup_band(0), landed, stage_recv).start()
        each(1, NZ, rootp_copy, lambda c: c.start())
        pltpu.make_async_copy(pan_src(0), pan_block(core, 0), pan_own).start()

    for c in range(2):
        ahead(0, piece(z, x_hi, core, 0), c, band(tgt, core * 2, c)).start()
        behind(0, piece(z, x_hi, core, 1), c, band(tgt, core * 2 + 1, c)).start()
        over(0, piece(z, x_hi, core, x_lo), c, band(tgt, core * 2 + x_lo, c)).start()
    side = 2 * x_lo - 1

    def take_over(t, c):
        p = piece(z - side * t, 1 - x_hi, core, 1 - x_lo)
        arrived(p, c)
        hand(t, p, c).start()
        share(p, c)

    def take_by(t, c):
        p = piece(z + side * t, 1 - x_hi, core, x_lo)
        arrived(p, c)
        share(p, c)

    def ring(u, carry):
        t, c = u // 2, u % 2
        p0 = piece(z - t, x_hi, core, 0)
        p1 = piece(z + t, x_hi, core, 1)
        arrived(p0, c)

        @pl.when(t < NZ - 1)
        def _():
            ahead(t, p0, c, held(p0, c)).start()

        arrived(p1, c)

        @pl.when(t < NZ - 1)
        def _():
            behind(t, p1, c, held(p1, c)).start()

        pc = piece(z + side * t, x_hi, core, x_lo)
        over(t, pc, c, held(pc, c)).start()
        share(p0, c)
        share(p1, c)
        take_over(t - 1, c)

        @pl.when(t >= 2)
        def _():
            take_by(t - 2, c)

        return carry

    own_piv = copy(piv_block(core, y, z), piv_block(core, y, z), px_send.at[0], piv_own, sibling)
    own_pan = copy(pan_block(core, z), pan_block(core, z), pxp_send.at[0], pan_own, sibling)

    def stage_begin():
        @pl.when(is_first & (y == 0))
        def _():
            pltpu.make_async_copy(sup_band(0), landed, stage_recv).wait()
            each(1, NY, line_copy, lambda c: c.start())
            pltpu.make_async_copy(staged(0), piv_block(core, 0, z), piv_own).start()
            own_pan.wait_recv()
            each(1, NY, linep_copy, lambda c: c.start())

    def stage_first():
        @pl.when(is_first)
        def _():
            own_piv.wait_recv()
            each(1, NX, x_copy, lambda c: c.start())
            each(1, NZ, z_copy, lambda c: c.start())

    def stage_other():
        @pl.when(x != first_x(z))
        def _():
            own_piv.wait_recv()
            each(1, NZ, z_copy, lambda c: c.start())

    def from_z(i):
        zz = (z + i) % NZ
        return copy(piv_block(core, y, zz), piv_block(core, y, zz), pz_send.at[i], piv_z.at[zz], sibling)

    def fromp_z(i):
        zz = (z + i) % NZ
        return copy(pan_block(core, zz), pan_block(core, zz), pzp_send.at[i], pan_z.at[zz], sibling)

    def stage_line():
        each(1, NZ, from_z, lambda c: c.wait_recv())
        for c in range(2):
            y_copy(0, 0, c).start()
            y_copy(1, 0, c).start()
        for c in range(2):
            b_copy(y, c).start()

        @pl.when(is_first & (y > 0))
        def _():
            own_pan.wait_recv()

        @pl.when(is_first)
        def _():
            each(1, NX, xp_copy, lambda c: c.start())

        @pl.when(x != first_x(z))
        def _():
            own_pan.wait_recv()

        each(1, NZ, zp_copy, lambda c: c.start())

    def y_step(t):
        for c in range(2):
            for way in range(2):
                if t < NY // 2 or c == way:
                    one = y_copy(way, t, c)
                    one.wait_recv()
                    if t < NY // 2 - 1 or (t == NY // 2 - 1 and c == way):
                        one.start()
                    b_copy((y + NY - t) % NY if way == 0 else (y + t) % NY, c).start()

    def ring_end(u):
        t, c = u // 2, u % 2
        take_over(t - 1, c)
        take_by(t - 2, c)

    stages = [(BEGIN_AT, stage_begin), (FIRST_AT, stage_first), (OTHER_AT, stage_other), (LINE_AT, stage_line)]
    stages += [(at, functools.partial(y_step, 1 + n)) for n, at in enumerate(LINE_STEPS)]
    done = 2
    for at, stage in sorted(stages, key=lambda one: one[0]):
        upto = min(at, 2 * NZ)
        if upto > done:
            lax.fori_loop(done, upto, lambda u, carry: ring(u, carry), 0)
            done = upto
        while done < at:
            if done < 2 * NZ + 2:
                ring_end(done)
            done += 1
        if at < 100:
            stage()
    for u in range(done, 2 * NZ + 2):
        ring_end(u)
    for c in range(2):
        take_by(NZ - 1, c)

    def sibling_target(i, carry):
        s = (col + i) % (2 * NZ)
        for q in range(2):
            for c in range(2):
                arrived(s * 4 + (1 - core) * 2 + q, c)
        return carry

    lax.fori_loop(1, 2 * NZ, sibling_target, 0)
    for one in loads:
        one.wait()

    chunk = 256
    chunks = full.shape[0] // chunk

    def rows_of(i):
        return pl.ds(pl.multiple_of(i * chunk, chunk), chunk)

    def strip(i, carry):
        kern[rows_of(i), :] = jnp.exp(scale * dot_t(full[rows_of(i), :], sup[...]))
        return carry

    def from_b(yy, c):
        return copy(piv_half(1 - core, yy, c), piv_half(1 - core, yy, c), pb_send.at[yy, c], piv_b.at[yy, c], sibling)

    for i in range(chunks):
        for n, at in enumerate(LINE_STEPS):
            if at == 100 + i:
                y_step(1 + n)
        strip(i, 0)
        if i == 1:
            each(1, NZ, fromp_z, lambda c: c.wait_recv())
            bp_copy().start()
    each(0, 2 * NY, lambda i: from_b(i // 2, i % 2), lambda c: c.wait_recv())
    copy(cross_pan.at[1 - core], cross_pan.at[1 - core], pbp_send, pan_b, sibling).wait_recv()

    span = sup.shape[0]
    here = pl.ds(pl.multiple_of(col * span, span), span)

    def out_copy(c):
        return copy(
            sol.at[pl.ds(pl.multiple_of(c * mine, mine), mine), :],
            out.at[:, here], out_send.at[c], out_recv.at[col], (row, c),
        )

    step_rows = STEP_ROWS
    steps = full.shape[0] // step_rows

    def solve(i, carry):
        number = (z * 2 * mine // step_rows + steps // 2 + i) % steps
        these = pl.ds(pl.multiple_of(number * step_rows, step_rows), step_rows)

        total = jnp.zeros((step_rows, 2 * width), jnp.float32)
        for yy in range(NY):
            total += dot_t(full[these, yy * part : (yy + 1) * part], piv[yy])
        pivots = jnp.exp(scale * total)
        first = dot_t(pivots[:, :width], inv[0], HIGH)
        left = pivots[:, width:] - jnp.dot(
            first, cross_pan[1], precision=HIGH, preferred_element_type=jnp.float32
        )
        second = dot_t(left, inv[1], HIGH)
        done = (
            kern[these, :]
            - jnp.dot(
                jnp.concatenate([first, second], axis=1), pan[...].reshape(2 * width, span),
                precision=HIGH, preferred_element_type=jnp.float32,
            )
        )
        head = jnp.where(
            (row == 0) & (col == 0), first,
            jnp.where((row == 1) & (col == 0), second, done[:, :width]),
        )
        sol[these, :width] = head
        sol[these, width:] = done[:, width:]
        for j in range(step_rows // mine):
            c = number * (step_rows // mine) + j

            @pl.when(c != col)
            def _():
                out_copy(c).start()

            @pl.when(c == col)
            def _():
                pltpu.make_async_copy(
                    sol.at[pl.ds(pl.multiple_of(c * mine, mine), mine), :],
                    out.at[:, here], out_recv.at[col],
                ).start()

        return carry

    lax.fori_loop(0, steps, solve, 0)

    def end_ring(u, carry):
        t, c = u // 2, u % 2
        ahead(t, 0, c, held(0, c)).wait_send()
        behind(t, 0, c, held(0, c)).wait_send()
        return carry

    lax.fori_loop(0, 2 * NZ - 2, end_ring, 0)

    def end_x(u, carry):
        t, c = u // 2, u % 2
        over(t, 0, c, held(0, c)).wait_send()
        hand(t, 0, c).wait_send()
        return carry

    lax.fori_loop(0, 2 * NZ, end_x, 0)

    def end_share(i, carry):
        s = (col + i) % (2 * NZ)
        for q in range(2):
            for c in range(2):
                sib(s * 4 + core * 2 + q, c).wait_send()
        return carry

    lax.fori_loop(1, 2 * NZ, end_share, 0)

    @pl.when(is_root)
    def _():
        each(1, NZ, root_copy, lambda c: c.wait_send())
        each(1, NZ, rootp_copy, lambda c: c.wait_send())

    @pl.when(is_first & (y == 0))
    def _():
        each(1, NY, line_copy, lambda c: c.wait_send())
        each(1, NY, linep_copy, lambda c: c.wait_send())

    @pl.when(is_first)
    def _():
        each(1, NX, x_copy, lambda c: c.wait_send())
        each(1, NX, xp_copy, lambda c: c.wait_send())

    each(1, NZ, z_copy, lambda c: c.wait_send())
    each(1, NZ, zp_copy, lambda c: c.wait_send())
    for t in range(NY // 2):
        for c in range(2):
            for way in range(2):
                if t < NY // 2 - 1 or c == way:
                    y_copy(way, t, c).wait_send()
    each(0, 2 * NY, lambda i: b_copy(i // 2, i % 2), lambda c: c.wait_send())
    bp_copy().wait_send()

    def end_out(i, carry):
        c = (col + i) % (2 * NZ)
        out_copy(c).wait_send()
        copy(
            sol.at[pl.ds(0, mine), :],
            out.at[:, pl.ds(pl.multiple_of(c * span, span), span)],
            out_send.at[c], out_recv.at[c], (row, c),
        ).wait_recv()
        return carry

    lax.fori_loop(1, 2 * NZ, end_out, 0)
    pltpu.make_async_copy(
        sol.at[pl.ds(pl.multiple_of(col * mine, mine), mine), :], out.at[:, here], out_recv.at[col]
    ).wait()


def shards(support, targets, panels, diag_inverses):
    span, feat = support.shape
    mine = targets.shape[0]
    width = diag_inverses.shape[1]
    n_col = 2 * NZ
    scale = 0.5 / math.sqrt(feat)
    dma = pltpu.SemaphoreType.DMA

    def kernel(*refs):
        body(scale, *refs)

    return pl.pallas_call(
        kernel,
        out_shape=jax.ShapeDtypeStruct((mine, span * n_col), jnp.float32),
        in_specs=[pl.BlockSpec(memory_space=pltpu.HBM)] * 4,
        out_specs=pl.BlockSpec(memory_space=pltpu.HBM),
        scratch_shapes=[
            pltpu.VMEM(support.shape, support.dtype),
            pltpu.VMEM(panels.shape, panels.dtype),
            pltpu.VMEM(diag_inverses.shape, diag_inverses.dtype),
            pltpu.VMEM((mine * n_col, feat), jnp.bfloat16),
            pltpu.VMEM((NY, 2 * width, feat // NY), jnp.bfloat16),
            pltpu.VMEM((2, width, width), jnp.float32),
            pltpu.VMEM((mine * n_col, span), jnp.float32),
            pltpu.VMEM((mine * n_col, span), jnp.float32),
            dma((4,)), dma((4 * n_col, 2)), dma((2, NZ, 2)), dma((NZ, 2)), dma((NZ, 2)), dma((4 * n_col, 2)),
            pltpu.VMEM((BAND, feat), jnp.bfloat16), dma, dma((NY,)), dma((NY,)),
            dma, dma((NZ,)), dma((NY, 2)), dma((NY, 2)),
            dma((NZ,)), dma((NX,)), dma((NZ,)), dma((2, NY, 2)), dma((NY, 2)),
            dma, dma((NZ,)), dma, dma((NZ,)), dma((NX,)), dma((NZ,)), dma,
            dma((n_col,)), dma((n_col,)),
        ],
        compiler_params=pltpu.CompilerParams(
            collective_id=0, has_side_effects=True, vmem_limit_bytes=67_000_000
        ),
    )(support, targets, panels, diag_inverses)


def solution(mesh):
    in_specs = (P(("row", "col"), None), P("col", None), P(None, None, ("row", "col")), P())
    out_specs = P("col", "row")
    return jax.shard_map(shards, mesh=mesh, in_specs=in_specs, out_specs=out_specs, check_vma=False)
```
